32 devices in a mesh: ax: 16 (over z, y, x), az: 2 (over core).
Axes of the slice: x: 2, y: 2, z: 4, core: 2. Of those that a mesh axis runs over, the one named last changes fastest.
Arguments:
- source: bfloat16 [2048, 512, 256], P(('ax', 'az')), may hold values from -6 to 6
- forcing: bfloat16 [2048, 512, 256], P(('ax', 'az')), may hold values from -6 to 6
- radial_basis: bfloat16 [128, 256, 256], P('az'), may hold values from -0.375 to 0.375
- eigenvalues: float32 [128, 256], P('az'), may hold values from 0.25 to 16
- radial_weight: float32 [256], replicated, may hold values from 0.5 to 2
Outputs:
- pressure: bfloat16 [2048, 512, 256], P(('ax', 'az'))
- velocity: bfloat16 [2048, 512, 256], P(('ax', 'az'))
The draws below stay inside these ranges and needn't reach their ends.
All inputs are finite; a program needn't handle non-finite values.
Results may differ from the reference program's by a relative error of at most 0.012.
Values may be sent and summed in bfloat16 or wider, within the bound.
A program may use at most 256 MiB of HBM per device.

```python
import math
import jax
import jax.numpy as jnp
from jax import lax

NZ = 2048
NTH = 512
NR = 256
KZ = 1024
NC = 256
MODES = 128


def steps_of(own_key, shape, cuts, smallest, high):
    factor_of = 1.0
    for dim, shards_of in cuts:
        draws = jax.random.uniform(jax.random.fold_in(jax.random.fold_in(own_key, 6), dim), (shards_of,), jnp.float32, smallest / len(cuts), high / len(cuts))
        factor_of = factor_of * jnp.repeat(jnp.exp(draws), shape[dim] // shards_of).reshape((-1,) + (1,) * (len(shape) - 1 - dim))
    return factor_of


def scatter_about(key, extent, spread, bound, cuts=(), kind=jnp.bfloat16):
    level = steps_of(key, extent, cuts, -0.22, 0.18) if cuts else 1.0
    result = jax.random.normal(key, extent, jnp.float32) * spread * level
    return jnp.minimum(jnp.maximum(result, -bound), bound).astype(kind)


def setup_inputs(seed: int = 0) -> dict:
    keys = jax.random.split(jax.random.key(seed), 6)
    return {
        "source": scatter_about(keys[0], (NZ, NTH, NR), 1.0, 6.0, ((0, 32),)),
        "forcing": scatter_about(keys[1], (NZ, NTH, NR), 1.0, 6.0, ((0, 32),)),
        "radial_basis": scatter_about(keys[2], (MODES, NR, NR), NR ** -0.5, 0.375, ((0, 2),)),
        "eigenvalues": jnp.clip(jnp.exp(math.log(16.0) - 4.158883 * jax.random.uniform(keys[3], (MODES, NR), jnp.float32) ** steps_of(keys[3], (MODES, NR), ((0, 2),), -0.2, 0.2)), 0.25, 16.0),
        "radial_weight": jnp.clip(jnp.exp(jax.random.uniform(keys[4], (NR,), jnp.float32, math.log(0.5), math.log(2.0))), 0.5, 2.0),
    }


VISCOUS = 0.5

def fourier_table(coef_count, point_count):
    slot_index = jnp.arange(coef_count, dtype=jnp.int32)
    frequency = jnp.where(slot_index == 1, coef_count // 2, slot_index // 2)
    sine_row = (slot_index % 2 == 1) & (slot_index != 1)
    grid_points = jnp.arange(point_count, dtype=jnp.int32)
    phase_index = frequency[:, None] * grid_points[None, :] % point_count
    angles = phase_index.astype(jnp.float32) * (2.0 * math.pi / point_count)
    table_values = jnp.where(sine_row[:, None], jnp.sin(angles), jnp.cos(angles)) * math.sqrt(2.0 / point_count)
    return table_values.astype(jnp.bfloat16)

def reference(source, forcing, radial_basis, eigenvalues, radial_weight):
    az_table = fourier_table(NC, NTH)
    axial_table = fourier_table(KZ, NZ)

    def to_coef(plane_data):
        return jnp.dot(az_table, plane_data, preferred_element_type=jnp.float32).astype(jnp.bfloat16)
    source_coef = lax.map(to_coef, source)
    forcing_coef = lax.map(to_coef, forcing)
    weighted = (radial_weight[None, :, None] * radial_basis.astype(jnp.float32)).astype(jnp.bfloat16)
    wavenumber = (jnp.arange(KZ, dtype=jnp.int32) // 2).astype(jnp.float32) * (8.0 / KZ)
    wave_sq = (wavenumber * wavenumber)[:, None]
    pair_wave = wavenumber[0::2][:, None]

    def per_coef(inputs):
        source_col, forcing_col, slot_index = inputs
        pair_slot = slot_index // 2
        basis_one = radial_basis[pair_slot]
        weighted_one = weighted[pair_slot]
        eigen_one = eigenvalues[pair_slot]
        source_hat = jnp.dot(axial_table, source_col, preferred_element_type=jnp.float32).astype(jnp.bfloat16)
        forcing_hat = jnp.dot(axial_table, forcing_col, preferred_element_type=jnp.float32).astype(jnp.bfloat16)
        transformed = jnp.dot(source_hat, weighted_one, preferred_element_type=jnp.float32)
        scaled = (transformed / (eigen_one[None, :] + wave_sq)).astype(jnp.bfloat16)
        pressure_full = jnp.dot(scaled, basis_one.T, preferred_element_type=jnp.float32)
        paired = pressure_full.reshape(KZ // 2, 2, NR)
        gradient = jnp.stack([pair_wave * paired[:, 1], -pair_wave * paired[:, 0]], axis=1).reshape(KZ, NR)
        helm_rhs = (forcing_hat.astype(jnp.float32) - gradient).astype(jnp.bfloat16)
        transformed_visc = jnp.dot(helm_rhs, weighted_one, preferred_element_type=jnp.float32)
        scaled_visc = (transformed_visc / (1.0 + VISCOUS * (eigen_one[None, :] + wave_sq))).astype(jnp.bfloat16)
        velocity_hat = jnp.dot(scaled_visc, basis_one.T, preferred_element_type=jnp.float32).astype(jnp.bfloat16)
        pressure_hat = pressure_full.astype(jnp.bfloat16)
        pressure_col = jnp.dot(axial_table.T, pressure_hat, preferred_element_type=jnp.float32).astype(jnp.bfloat16)
        velocity_col = jnp.dot(axial_table.T, velocity_hat, preferred_element_type=jnp.float32).astype(jnp.bfloat16)
        return (pressure_col, velocity_col)
    pressure_cols, velocity_cols = lax.map(per_coef, (source_coef.transpose(1, 0, 2), forcing_coef.transpose(1, 0, 2), jnp.arange(NC, dtype=jnp.int32)))

    def to_grid(plane_data):
        return jnp.dot(az_table.T, plane_data, preferred_element_type=jnp.float32).astype(jnp.bfloat16)
    pressure = lax.map(to_grid, pressure_cols.transpose(1, 0, 2))
    velocity = lax.map(to_grid, velocity_cols.transpose(1, 0, 2))
    return (pressure, velocity)
```

```python
import functools
import math

import jax
import jax.numpy as jnp
from jax import lax
from jax.experimental import pallas as pl
from jax.experimental.layout import Layout, with_layout_constraint
from jax.experimental.pallas import tpu as pltpu
from jax.sharding import PartitionSpec as P

VISCOUS = 0.5
LENGTH = 8.0


def fourier_table(coef_count, point_count):
    slot_index = jnp.arange(coef_count, dtype=jnp.int32)
    frequency = jnp.where(slot_index == 1, coef_count // 2, slot_index // 2)
    sine_row = (slot_index % 2 == 1) & (slot_index != 1)
    grid_points = jnp.arange(point_count, dtype=jnp.int32)
    phase_index = frequency[:, None] * grid_points[None, :] % point_count
    angles = phase_index.astype(jnp.float32) * (2.0 * math.pi / point_count)
    table_values = jnp.where(sine_row[:, None], jnp.sin(angles), jnp.cos(angles)) * math.sqrt(
        2.0 / point_count
    )
    return table_values.astype(jnp.bfloat16)


def plane_block(plane_count):
    return 8 if plane_count % 8 == 0 else 1


def coef_kernel(ax_count, az_count, coef_local, table_ref, plane_ref, out_ref):
    planes, _, radial = plane_ref.shape
    half = ax_count * coef_local
    for z in range(planes):
        coefs = jnp.dot(table_ref[...], plane_ref[z], preferred_element_type=jnp.float32)
        for part in range(az_count):
            rows = coefs[part * half : (part + 1) * half]
            out_ref[:, part, z] = rows.reshape(ax_count, coef_local, radial).astype(out_ref.dtype)


def to_coef(table, planes, ax_count, az_count):
    coef_count, point_count = table.shape
    plane_count, _, radial = planes.shape
    coef_local = coef_count // (ax_count * az_count)
    block = plane_block(plane_count)
    return pl.pallas_call(
        functools.partial(coef_kernel, ax_count, az_count, coef_local),
        grid=(plane_count // block,),
        in_specs=[
            pl.BlockSpec((coef_count, point_count), lambda i: (0, 0)),
            pl.BlockSpec((block, point_count, radial), lambda i: (i, 0, 0)),
        ],
        out_specs=pl.BlockSpec(
            (ax_count, az_count, block, coef_local, radial), lambda i: (0, 0, i, 0, 0)
        ),
        out_shape=jax.ShapeDtypeStruct(
            (ax_count, az_count, plane_count, coef_local, radial), jnp.bfloat16
        ),
        cost_estimate=pl.CostEstimate(
            flops=2 * plane_count * coef_count * point_count * radial,
            bytes_accessed=2 * plane_count * (coef_count + point_count) * radial,
            transcendentals=0,
        ),
        compiler_params=pltpu.CompilerParams(vmem_limit_bytes=56 * 2**20),
        name="to_coef",
    )(table, planes)


def grid_kernel(ax_count, az_count, coef_local, table_ref, coef_ref, out_ref):
    planes, _, radial = out_ref.shape
    half = ax_count * coef_local
    for z in range(planes):
        parts = [
            coef_ref[:, part, z].astype(jnp.float32).reshape(half, radial)
            for part in range(az_count)
        ]
        coefs = jnp.concatenate(parts, axis=0).astype(jnp.bfloat16)
        out_ref[z] = jnp.dot(
            table_ref[...], coefs, preferred_element_type=jnp.float32
        ).astype(out_ref.dtype)


def to_grid(table_t, coefs):
    point_count, coef_count = table_t.shape
    ax_count, az_count, plane_count, coef_local, radial = coefs.shape
    block = plane_block(plane_count)
    return pl.pallas_call(
        functools.partial(grid_kernel, ax_count, az_count, coef_local),
        grid=(plane_count // block,),
        in_specs=[
            pl.BlockSpec((point_count, coef_count), lambda i: (0, 0)),
            pl.BlockSpec(
                (ax_count, az_count, block, coef_local, radial), lambda i: (0, 0, i, 0, 0)
            ),
        ],
        out_specs=pl.BlockSpec((block, point_count, radial), lambda i: (i, 0, 0)),
        out_shape=jax.ShapeDtypeStruct((plane_count, point_count, radial), jnp.bfloat16),
        cost_estimate=pl.CostEstimate(
            flops=2 * plane_count * coef_count * point_count * radial,
            bytes_accessed=2 * plane_count * (coef_count + point_count) * radial,
            transcendentals=0,
        ),
        compiler_params=pltpu.CompilerParams(vmem_limit_bytes=56 * 2**20),
        name="to_grid",
    )(table_t, coefs)


def per_device(source, forcing, radial_basis, eigenvalues, radial_weight):
    ax_count = lax.axis_size("ax")
    az_count = lax.axis_size("az")
    device_count = ax_count * az_count
    plane_local, point_count, radial = source.shape
    plane_count = plane_local * device_count
    coef_count = 2 * radial_basis.shape[0] * az_count
    wave_count = plane_count // 2
    coef_local = coef_count // device_count
    az_table = fourier_table(coef_count, point_count)

    def exchange(blocks):
        flat = blocks.reshape(device_count, plane_local, coef_local, radial)
        return lax.all_to_all(flat, ("ax", "az"), split_axis=0, concat_axis=0, tiled=True)

    def to_owner(planes):
        received = exchange(to_coef(az_table, planes, ax_count, az_count))
        return received.reshape(plane_count, coef_local, radial)

    def to_planes(cols):
        received = exchange(cols)
        blocks = received.reshape(ax_count, az_count, plane_local, coef_local, radial)
        return to_grid(az_table.T, blocks)

    source_blocks = to_coef(az_table, source, ax_count, az_count)
    source_cols = exchange(source_blocks).reshape(plane_count, coef_local, radial)
    forcing_cols = to_owner(forcing)
    axial_table = lax.optimization_barrier(fourier_table(wave_count, plane_count))

    first_coef = lax.axis_index("ax") * coef_local
    pair_index = (first_coef + jnp.arange(coef_local, dtype=jnp.int32)) // 2
    basis_rows = jnp.take(radial_basis, pair_index, axis=0)
    eigen_rows = jnp.take(eigenvalues, pair_index, axis=0)[:, None, :]
    weighted_rows = (radial_weight[None, :, None] * basis_rows.astype(jnp.float32)).astype(
        jnp.bfloat16
    )
    wave_index = jnp.arange(wave_count, dtype=jnp.int32)
    wavenumber = (wave_index // 2).astype(jnp.float32) * (LENGTH / wave_count)
    wave_sq = (wavenumber * wavenumber)[None, :, None]

    def axial(cols):
        return jnp.einsum(
            "kz,zcr->kcr", axial_table, cols, preferred_element_type=jnp.float32
        ).astype(jnp.bfloat16).transpose(1, 0, 2)

    def axial_back(hat):
        return jnp.einsum(
            "kz,ckr->zcr", axial_table, hat, preferred_element_type=jnp.float32
        ).astype(jnp.bfloat16)

    def transform(hat):
        return jnp.einsum(
            "ckr,crj->ckj", hat, weighted_rows, preferred_element_type=jnp.float32
        )

    def back(scaled):
        return jnp.einsum(
            "ckj,crj->ckr", scaled, basis_rows, preferred_element_type=jnp.float32
        )

    scaled = (transform(axial(source_cols)) / (eigen_rows + wave_sq)).astype(jnp.bfloat16)
    pressure_full = back(scaled)
    pressure_cols = with_layout_constraint(
        axial_back(pressure_full.astype(jnp.bfloat16)), Layout(major_to_minor=(0, 1, 2))
    )
    pressure_blocks, forcing_cols = lax.optimization_barrier((pressure_cols, forcing_cols))
    pressure = to_planes(pressure_blocks)

    paired = pressure_full.reshape(coef_local, wave_count // 2, 2, radial)
    pair_wave = wavenumber.reshape(wave_count // 2, 2)[:, 0][None, :, None]
    gradient = jnp.stack(
        [pair_wave * paired[:, :, 1], -pair_wave * paired[:, :, 0]], axis=2
    ).reshape(pressure_full.shape)
    helm_rhs = (axial(forcing_cols).astype(jnp.float32) - gradient).astype(jnp.bfloat16)
    scaled_visc = (
        transform(helm_rhs) / (1.0 + VISCOUS * (eigen_rows + wave_sq))
    ).astype(jnp.bfloat16)
    velocity = to_planes(axial_back(back(scaled_visc).astype(jnp.bfloat16)))
    return (pressure, velocity)


def solution(mesh):
    placed = (
        P(("ax", "az"), None, None),
        P(("ax", "az"), None, None),
        P("az", None, None),
        P("az", None),
        P(),
    )
    return jax.shard_map(
        per_device,
        mesh=mesh,
        in_specs=placed,
        out_specs=(P(("ax", "az"), None, None), P(("ax", "az"), None, None)),
        check_vma=False,
    )
```
